512 devices in a mesh: outer: 16 (over z, core), inner: 32 (over x, y).
Axes of the slice: x: 4, y: 8, z: 8, core: 2. Of those that a mesh axis runs over, the one named last changes fastest.
Arguments:
- queries: bfloat16 [65536, 2048], P(('outer', 'inner')), may hold values from -6 to 6
- keys: bfloat16 [65536, 2048], P(('outer', 'inner')), may hold values from -6 to 6
- values: bfloat16 [65536, 2048], P(('outer', 'inner')), may hold values from -6 to 6
- cotangent: bfloat16 [65536, 2048], P(('outer', 'inner')), may hold values from -6 to 6
Outputs:
- attended: bfloat16 [65536, 2048], P(('outer', 'inner'))
- grad_queries: bfloat16 [65536, 2048], P(('outer', 'inner'))
- grad_keys: bfloat16 [65536, 2048], P(('outer', 'inner'))
- grad_values: bfloat16 [65536, 2048], P(('outer', 'inner'))
The draws below stay inside these ranges and needn't reach their ends.
All inputs are finite; a program needn't handle non-finite values.
Results may differ from the reference program's by a relative error of at most 0.013.
Values may be sent and summed in bfloat16 or wider, within the bound.
A program may use at most 64 MiB of HBM per device.

```python
import jax
import jax.numpy as jnp
from jax import lax

HEADS = 16
HEAD = 128
BLOCK = 512
HALF = 64
TOKENS = 65536


def level_of(rng, extent, split, least, high):
    loudness, own = 1.0, jax.random.fold_in(rng, 6)
    for axis_at, shards_of in split:
        draws = jnp.exp(jax.random.uniform(jax.random.fold_in(own, axis_at), (shards_of,), jnp.float32, least / len(split), high / len(split)))
        loudness = loudness * jnp.repeat(draws, extent[axis_at] // shards_of).reshape([-1 if axis == axis_at else 1 for axis in range(len(extent))])
    return loudness


def centred(own_key, shape, scale, limit, pieces=(), kind=jnp.bfloat16):
    array = scale * jax.random.normal(own_key, shape, jnp.float32)
    if pieces:
        array = array * level_of(own_key, shape, pieces, -0.22, 0.18)
    return jnp.clip(array, -limit, limit).astype(kind)


def setup_inputs(seed: int = 0) -> dict:
    arg_keys = jax.random.split(jax.random.key(seed), 5)
    queries = centred(arg_keys[0], (TOKENS, HEADS * HEAD), 1.0, 6.0, ((0, 512),))
    keys = centred(arg_keys[1], (TOKENS, HEADS * HEAD), 1.0, 6.0, ((0, 512),))
    values = centred(arg_keys[2], (TOKENS, HEADS * HEAD), 1.0, 6.0, ((0, 512),))
    cotangent = centred(arg_keys[3], (TOKENS, HEADS * HEAD), 1.0, 6.0, ((0, 512),))
    return {"queries": queries, "keys": keys, "values": values, "cotangent": cotangent}


def round_keep(x):
    return lax.optimization_barrier(x.astype(jnp.bfloat16)).astype(jnp.float32)


def reference(queries, keys, values, cotangent):
    scale = float(HEAD * TOKENS) ** -0.5
    nblocks = TOKENS // BLOCK
    qs = queries.reshape(nblocks, BLOCK, HEADS, HEAD)
    ks = keys.reshape(nblocks, BLOCK, HEADS, HEAD)
    vs = values.reshape(nblocks, BLOCK, HEADS, 2, HALF)
    ds = cotangent.reshape(nblocks, BLOCK, HEADS, 2, HALF)

    def totals(parts):
        qq, kk, vv, dd = [x.astype(jnp.float32) for x in parts]
        kv_sum = jnp.einsum('shk,shpv->hpkv', kk, vv)
        qd_sum = jnp.einsum('thk,thpv->hpkv', qq, dd)
        return kv_sum, qd_sum

    kv_blocks, qd_blocks = lax.map(totals, (qs, ks, vs, ds))
    s_before = jnp.cumsum(kv_blocks, 0) - kv_blocks
    g_after = jnp.sum(qd_blocks, 0)[None] - jnp.cumsum(qd_blocks, 0)
    lower = jnp.arange(BLOCK)[:, None] >= jnp.arange(BLOCK)[None, :]

    def one_block(parts):
        qq, kk, vv, dd, state, adjoint = parts
        qq = qq.astype(jnp.float32)
        kk = kk.astype(jnp.float32)
        vv = vv.astype(jnp.float32)
        dd = dd.astype(jnp.float32)
        s_round = round_keep(state)
        g_round = round_keep(adjoint)
        scores = jnp.einsum('thk,shk->hts', qq, kk)
        a_round = round_keep(jnp.where(lower[None], scores, 0.0))
        back = jnp.einsum('thpv,shpv->hpts', dd, vv)
        b_round = round_keep(jnp.where(lower[None, None], back, 0.0))
        attended = scale * (jnp.einsum('thk,hpkv->thpv', qq, s_round) + jnp.einsum('hts,shpv->thpv', a_round, vv))
        grad_q = scale * (jnp.einsum('thpv,hpkv->thk', dd, s_round) + jnp.einsum('hpts,shk->thk', b_round, kk))
        grad_k = scale * (jnp.einsum('shpv,hpkv->shk', vv, g_round) + jnp.einsum('hpts,thk->shk', b_round, qq))
        grad_v = scale * (jnp.einsum('shk,hpkv->shpv', kk, g_round) + jnp.einsum('hts,thpv->shpv', a_round, dd))
        return (attended.astype(jnp.bfloat16), grad_q.astype(jnp.bfloat16),
                grad_k.astype(jnp.bfloat16), grad_v.astype(jnp.bfloat16))

    attended, grad_q, grad_k, grad_v = lax.map(one_block, (qs, ks, vs, ds, s_before, g_after))
    width = HEADS * HEAD
    return (attended.reshape(TOKENS, width), grad_q.reshape(TOKENS, width),
            grad_k.reshape(TOKENS, width), grad_v.reshape(TOKENS, width))
```

```python
import functools

import jax
import jax.numpy as jnp
from jax import lax
from jax.experimental import pallas as pl
from jax.experimental.pallas import tpu as pltpu
from jax.sharding import PartitionSpec as P

HEAD = 128


def dot(a, b, over_a, over_b):
    return lax.dot_general(
        a, b, (((over_a,), (over_b,)), ((), ())), preferred_element_type=jnp.float32
    )


def states_kernel(heads, q_ref, k_ref, v_ref, d_ref, out_ref):
    for h in range(heads):
        cols = slice(h * HEAD, (h + 1) * HEAD)
        out_ref[h] = dot(k_ref[:, cols], v_ref[:, cols], 0, 0).astype(out_ref.dtype)
        out_ref[heads + h] = dot(q_ref[:, cols], d_ref[:, cols], 0, 0).astype(out_ref.dtype)


def outputs_kernel(heads, scale, q_ref, k_ref, v_ref, d_ref, s_ref, o_ref, gq_ref, gk_ref, gv_ref):
    rows = q_ref.shape[0]
    lower = lax.broadcasted_iota(jnp.int32, (rows, rows), 0) >= lax.broadcasted_iota(
        jnp.int32, (rows, rows), 1
    )
    for h in range(heads):
        cols = slice(h * HEAD, (h + 1) * HEAD)
        q, k, v, d = q_ref[:, cols], k_ref[:, cols], v_ref[:, cols], d_ref[:, cols]
        s, g = s_ref[h], s_ref[heads + h]
        a = jnp.where(lower, dot(q, k, 1, 1), 0.0).astype(jnp.bfloat16)
        b = jnp.where(lower, dot(d, v, 1, 1), 0.0).astype(jnp.bfloat16)
        o_ref[:, cols] = (scale * (dot(q, s, 1, 0) + dot(a, v, 1, 0))).astype(o_ref.dtype)
        gq_ref[:, cols] = (scale * (dot(d, s, 1, 1) + dot(b, k, 1, 0))).astype(gq_ref.dtype)
        gk_ref[:, cols] = (scale * (dot(v, g, 1, 1) + dot(b, q, 0, 0))).astype(gk_ref.dtype)
        gv_ref[:, cols] = (scale * (dot(k, g, 1, 0) + dot(a, d, 0, 0))).astype(gv_ref.dtype)


def body(queries, keys, values, cotangent):
    rows, width = queries.shape
    heads = width // HEAD
    inner, outer = lax.axis_size("inner"), lax.axis_size("outer")
    scale = float(HEAD * rows * inner * outer) ** (-0.5)
    slabs = 2 * heads
    own = slabs // inner
    vmem = pl.BlockSpec(memory_space=pltpu.VMEM)

    states = pl.pallas_call(
        functools.partial(states_kernel, heads),
        out_shape=jax.ShapeDtypeStruct((slabs, HEAD, HEAD), jnp.bfloat16),
        in_specs=[vmem] * 4,
        out_specs=vmem,
    )(queries, keys, values, cotangent)

    arrived = lax.all_to_all(states, "inner", split_axis=0, concat_axis=0, tiled=True)
    arrived = arrived.reshape(inner, own, HEAD, HEAD)
    slab = lax.axis_index("inner") * own
    before = slab < heads
    at = jnp.arange(inner)
    reach = jnp.where(before, at[None, :] < at[:, None], at[None, :] > at[:, None])
    within = jnp.einsum(
        "ij,jukv->iukv", reach.astype(jnp.bfloat16), arrived, preferred_element_type=jnp.float32
    )
    total = jnp.sum(arrived.astype(jnp.float32), 0)
    everything = lax.all_gather(total, "outer")
    place, group = lax.axis_index("outer"), jnp.arange(outer)
    reached = jnp.where(before, group < place, group > place)
    carried = jnp.sum(jnp.where(reached[:, None, None, None], everything, 0.0), 0)
    whole = (within + carried[None]).astype(jnp.bfloat16).reshape(slabs, HEAD, HEAD)
    state = lax.all_to_all(whole, "inner", split_axis=0, concat_axis=0, tiled=True)

    return pl.pallas_call(
        functools.partial(outputs_kernel, heads, scale),
        out_shape=(jax.ShapeDtypeStruct((rows, width), jnp.bfloat16),) * 4,
        in_specs=[vmem] * 5,
        out_specs=(vmem,) * 4,
    )(queries, keys, values, cotangent, state)


def solution(mesh):
    spec = P(("outer", "inner"), None)
    return jax.shard_map(
        body, mesh=mesh, in_specs=(spec,) * 4, out_specs=(spec,) * 4, check_vma=False
    )
```

```python
import functools

import jax
import jax.numpy as jnp
from jax import lax
from jax.experimental import pallas as pl
from jax.experimental.pallas import tpu as pltpu
from jax.sharding import PartitionSpec as P

HEAD = 128
MESH = pl.DeviceIdType.MESH


def dot(a, b, over_a, over_b):
    return lax.dot_general(
        a, b, (((over_a,), (over_b,)), ((), ())), preferred_element_type=jnp.float32
    )


def exchange_kernel(
    heads, inner, outer, q_ref, k_ref, v_ref, d_ref, state_ref,
    states, arrived, prefix, outgoing, total, mate, pair, pairs, carried,
    in_send, in_recv, z_send, z_recv, out_send, out_recv, core_send, core_recv,
):
    me, place = lax.axis_index("inner"), lax.axis_index("outer")
    chips, half = outer // 2, HEAD // 2
    z, core = place // 2, place % 2
    other = (place + 1 - 2 * core, me)
    later = me // heads
    my_rows = pl.ds(pl.multiple_of(core * half, half), half)
    other_rows = pl.ds(pl.multiple_of((1 - core) * half, half), half)

    def in_copy(peer, source):
        return pltpu.make_async_remote_copy(
            states.at[peer], arrived.at[source], in_send.at[peer], in_recv.at[source],
            device_id=(place, peer), device_id_type=MESH,
        )

    def z_copy(peer, source):
        return pltpu.make_async_remote_copy(
            pair, pairs.at[source], z_send.at[peer], z_recv.at[source],
            device_id=(peer * 2 + core, me), device_id_type=MESH,
        )

    def out_copy(peer, source):
        return pltpu.make_async_remote_copy(
            outgoing.at[peer], state_ref.at[source], out_send.at[peer], out_recv.at[source],
            device_id=(place, peer), device_id_type=MESH,
        )

    def total_copy():
        return pltpu.make_async_remote_copy(
            total, mate, core_send.at[0], core_recv.at[0], device_id=other, device_id_type=MESH
        )

    def carried_copy(rows):
        return pltpu.make_async_remote_copy(
            carried.at[rows], carried.at[rows], core_send.at[1], core_recv.at[1],
            device_id=other, device_id_type=MESH,
        )

    barrier = pltpu.get_barrier_semaphore()

    @pl.loop(1, inner)
    def _(step):
        pl.semaphore_signal(
            barrier, inc=1, device_id=(place, (me + step) % inner), device_id_type=MESH
        )

    @pl.loop(1, chips)
    def _(step):
        pl.semaphore_signal(
            barrier, inc=1, device_id=((z + step) % chips * 2 + core, me), device_id_type=MESH
        )

    pl.semaphore_signal(barrier, inc=1, device_id=other, device_id_type=MESH)

    for h in range(heads):
        cols = slice(h * HEAD, (h + 1) * HEAD)
        states[h] = dot(k_ref[:, cols], v_ref[:, cols], 0, 0).astype(states.dtype)
        states[heads + h] = dot(q_ref[:, cols], d_ref[:, cols], 0, 0).astype(states.dtype)

    pl.semaphore_wait(barrier, inner - 1 + chips - 1 + 1)

    @pl.loop(1, inner)
    def _(step):
        in_copy((me + step) % inner, me).start()

    own = states[me]
    arrived[me] = own

    def add_arrived(step, acc):
        source = (me + inner - step) % inner
        in_copy(source, source).wait_recv()
        return acc + arrived[source].astype(jnp.float32)

    total[...] = lax.fori_loop(1, inner, add_arrived, own.astype(jnp.float32))
    total_copy().start()

    def turn(step, acc):
        at = step + later * (inner - 1 - 2 * step)
        prefix[at] = acc
        return acc + arrived[at].astype(jnp.float32)

    lax.fori_loop(0, inner, turn, jnp.zeros((HEAD, HEAD), jnp.float32))

    total_copy().wait_recv()
    pair[...] = (total[my_rows] + mate[my_rows]).astype(pair.dtype)

    @pl.loop(1, chips)
    def _(step):
        z_copy((z + step) % chips, z).start()

    def add_pair(step, acc):
        source = (z + chips - step) % chips
        z_copy(source, source).wait_recv()
        reached = (source - z) * (2 * later - 1) > 0
        return acc + jnp.where(reached, pairs[source].astype(jnp.float32), 0.0)

    carried[my_rows] = lax.fori_loop(1, chips, add_pair, jnp.zeros((half, HEAD), jnp.float32))
    carried_copy(my_rows).start()
    carried_copy(other_rows).wait_recv()
    offset = carried[...] + jnp.where(core + later == 1, mate[...], 0.0)

    outgoing[me] = (prefix[me] + offset).astype(outgoing.dtype)
    state_ref[me] = (prefix[me] + offset).astype(outgoing.dtype)

    @pl.loop(1, inner)
    def _(step):
        peer = (me + step) % inner
        outgoing[peer] = (prefix[peer] + offset).astype(outgoing.dtype)
        out_copy(peer, me).start()

    @pl.loop(1, inner)
    def _(step):
        source = (me + inner - step) % inner
        out_copy(source, source).wait_recv()

    @pl.loop(1, inner)
    def _(step):
        peer = (me + step) % inner
        in_copy(peer, me).wait_send()
        out_copy(peer, me).wait_send()

    @pl.loop(1, chips)
    def _(step):
        z_copy((z + step) % chips, z).wait_send()

    total_copy().wait_send()
    carried_copy(my_rows).wait_send()


def outputs_kernel(heads, scale, q_ref, k_ref, v_ref, d_ref, s_ref, o_ref, gq_ref, gk_ref, gv_ref):
    rows = q_ref.shape[0]
    lower = lax.broadcasted_iota(jnp.int32, (rows, rows), 0) >= lax.broadcasted_iota(
        jnp.int32, (rows, rows), 1
    )
    for h in range(heads):
        cols = slice(h * HEAD, (h + 1) * HEAD)
        q, k, v, d = q_ref[:, cols], k_ref[:, cols], v_ref[:, cols], d_ref[:, cols]
        s, g = s_ref[h], s_ref[heads + h]
        a = jnp.where(lower, dot(q, k, 1, 1), 0.0).astype(jnp.bfloat16)
        b = jnp.where(lower, dot(d, v, 1, 1), 0.0).astype(jnp.bfloat16)
        o_ref[:, cols] = (scale * (dot(q, s, 1, 0) + dot(a, v, 1, 0))).astype(o_ref.dtype)
        gq_ref[:, cols] = (scale * (dot(d, s, 1, 1) + dot(b, k, 1, 0))).astype(gq_ref.dtype)
        gk_ref[:, cols] = (scale * (dot(v, g, 1, 1) + dot(b, q, 0, 0))).astype(gk_ref.dtype)
        gv_ref[:, cols] = (scale * (dot(k, g, 1, 0) + dot(a, d, 0, 0))).astype(gv_ref.dtype)


def body(queries, keys, values, cotangent):
    rows, width = queries.shape
    heads = width // HEAD
    inner, outer = lax.axis_size("inner"), lax.axis_size("outer")
    scale = float(HEAD * rows * inner * outer) ** (-0.5)
    slabs = 2 * heads
    assert slabs == inner
    chips, half = outer // 2, HEAD // 2
    vmem = pl.BlockSpec(memory_space=pltpu.VMEM)
    dma = pltpu.SemaphoreType.DMA

    state = pl.pallas_call(
        functools.partial(exchange_kernel, heads, inner, outer),
        out_shape=jax.ShapeDtypeStruct((slabs, HEAD, HEAD), jnp.bfloat16),
        in_specs=[vmem] * 4,
        out_specs=vmem,
        scratch_shapes=[
            pltpu.VMEM((slabs, HEAD, HEAD), jnp.bfloat16),
            pltpu.VMEM((slabs, HEAD, HEAD), jnp.bfloat16),
            pltpu.VMEM((slabs, HEAD, HEAD), jnp.float32),
            pltpu.VMEM((slabs, HEAD, HEAD), jnp.bfloat16),
            pltpu.VMEM((HEAD, HEAD), jnp.float32),
            pltpu.VMEM((HEAD, HEAD), jnp.float32),
            pltpu.VMEM((half, HEAD), jnp.bfloat16),
            pltpu.VMEM((chips, half, HEAD), jnp.bfloat16),
            pltpu.VMEM((HEAD, HEAD), jnp.float32),
            dma((inner,)), dma((inner,)), dma((chips,)), dma((chips,)),
            dma((inner,)), dma((inner,)), dma((2,)), dma((2,)),
        ],
        compiler_params=pltpu.CompilerParams(collective_id=0, has_side_effects=True),
    )(queries, keys, values, cotangent)

    return pl.pallas_call(
        functools.partial(outputs_kernel, heads, scale),
        out_shape=(jax.ShapeDtypeStruct((rows, width), jnp.bfloat16),) * 4,
        in_specs=[vmem] * 5,
        out_specs=(vmem,) * 4,
    )(queries, keys, values, cotangent, state)


def solution(mesh):
    spec = P(("outer", "inner"), None)
    return jax.shard_map(
        body, mesh=mesh, in_specs=(spec,) * 4, out_specs=(spec,) * 4, check_vma=False
    )
```

```python
import functools

import jax
import jax.numpy as jnp
from jax import lax
from jax.experimental import pallas as pl
from jax.experimental.pallas import tpu as pltpu
from jax.sharding import PartitionSpec as P

HEAD = 128
MESH = pl.DeviceIdType.MESH


def dot(a, b, over_a, over_b):
    return lax.dot_general(
        a, b, (((over_a,), (over_b,)), ((), ())), preferred_element_type=jnp.float32
    )


def exchange_kernel(
    heads, inner, outer, q_ref, k_ref, v_ref, d_ref, state_ref,
    states, arrived, prefix, outgoing, total, mate, pair, pairs, carried,
    in_send, in_recv, z_send, z_recv, out_send, out_recv, core_send, core_recv,
):
    me, place = lax.axis_index("inner"), lax.axis_index("outer")
    chips, half, quarter = outer // 2, HEAD // 2, HEAD // 4
    z, core = place // 2, place % 2
    other = (place + 1 - 2 * core, me)
    my_rows = pl.ds(pl.multiple_of(core * quarter, quarter), quarter)
    other_rows = pl.ds(pl.multiple_of((1 - core) * quarter, quarter), quarter)

    def in_copy(kind, peer, source):
        return pltpu.make_async_remote_copy(
            states.at[kind, peer], arrived.at[kind, source],
            in_send.at[kind, peer], in_recv.at[kind, source],
            device_id=(place, peer), device_id_type=MESH,
        )

    def z_copy(kind, peer, source):
        return pltpu.make_async_remote_copy(
            pair.at[kind], pairs.at[kind, source], z_send.at[kind, peer], z_recv.at[kind, source],
            device_id=(peer * 2 + core, me), device_id_type=MESH,
        )

    def state_at(kind, source):
        rows = pl.ds(pl.multiple_of(source // heads * half, half), half)
        return state_ref.at[kind, source % heads, rows]

    def out_copy(kind, peer, source):
        return pltpu.make_async_remote_copy(
            outgoing.at[kind, peer], state_at(kind, source),
            out_send.at[kind, peer], out_recv.at[kind, source],
            device_id=(place, peer), device_id_type=MESH,
        )

    def total_copy(kind):
        return pltpu.make_async_remote_copy(
            total.at[kind], mate.at[kind], core_send.at[0, kind], core_recv.at[0, kind],
            device_id=other, device_id_type=MESH,
        )

    def carried_copy(kind, rows):
        return pltpu.make_async_remote_copy(
            carried.at[kind, rows], carried.at[kind, rows],
            core_send.at[1, kind], core_recv.at[1, kind],
            device_id=other, device_id_type=MESH,
        )

    def make_states(kind, a_ref, b_ref):
        for h in range(heads):
            cols = slice(h * HEAD, (h + 1) * HEAD)
            both = dot(a_ref[:, cols], b_ref[:, cols], 0, 0).astype(states.dtype)
            states[kind, h] = both[:half]
            states[kind, heads + h] = both[half:]

    def send_states(kind):
        @pl.loop(1, inner)
        def _(step):
            in_copy(kind, (me + step) % inner, me).start()

        arrived[kind, me] = states[kind, me]

    def sum_within(kind):
        def add_arrived(step, acc):
            source = (me + inner - step) % inner
            in_copy(kind, source, source).wait_recv()
            return acc + arrived[kind, source].astype(jnp.float32)

        total[kind] = lax.fori_loop(1, inner, add_arrived, states[kind, me].astype(jnp.float32))
        total_copy(kind).start()

        def turn(step, acc):
            at = step if kind == 0 else inner - 1 - step
            prefix[kind, at] = acc
            return acc + arrived[kind, at].astype(jnp.float32)

        lax.fori_loop(0, inner, turn, jnp.zeros((half, HEAD), jnp.float32))

    def send_pair(kind):
        total_copy(kind).wait_recv()
        pair[kind] = (total[kind, my_rows] + mate[kind, my_rows]).astype(pair.dtype)

        @pl.loop(1, chips)
        def _(step):
            z_copy(kind, (z + step) % chips, z).start()

    def sum_across(kind):
        def add_pair(step, acc):
            source = (z + chips - step) % chips
            z_copy(kind, source, source).wait_recv()
            reached = source < z if kind == 0 else source > z
            return acc + jnp.where(reached, pairs[kind, source].astype(jnp.float32), 0.0)

        zeros = jnp.zeros((quarter, HEAD), jnp.float32)
        carried[kind, my_rows] = lax.fori_loop(1, chips, add_pair, zeros)
        carried_copy(kind, my_rows).start()
        carried_copy(kind, other_rows).wait_recv()

    def send_sums(kind):
        offset = carried[kind] + jnp.where(core + kind == 1, mate[kind], 0.0)

        @pl.loop(1, inner)
        def _(step):
            peer = (me + step) % inner
            outgoing[kind, peer] = (prefix[kind, peer] + offset).astype(outgoing.dtype)
            out_copy(kind, peer, me).start()

        state_at(kind, me)[...] = (prefix[kind, me] + offset).astype(outgoing.dtype)

    barrier = pltpu.get_barrier_semaphore()

    @pl.loop(1, inner)
    def _(step):
        pl.semaphore_signal(
            barrier, inc=1, device_id=(place, (me + step) % inner), device_id_type=MESH
        )

    @pl.loop(1, chips)
    def _(step):
        pl.semaphore_signal(
            barrier, inc=1, device_id=((z + step) % chips * 2 + core, me), device_id_type=MESH
        )

    pl.semaphore_signal(barrier, inc=1, device_id=other, device_id_type=MESH)
    make_states(0, k_ref, v_ref)
    pl.semaphore_wait(barrier, inner - 1 + chips - 1 + 1)
    send_states(0)
    make_states(1, q_ref, d_ref)
    send_states(1)
    for kind in range(2):
        sum_within(kind)
        send_pair(kind)
        sum_across(kind)
        send_sums(kind)

    for kind in range(2):

        @pl.loop(1, inner)
        def _(step):
            source = (me + inner - step) % inner
            out_copy(kind, source, source).wait_recv()

    for kind in range(2):

        @pl.loop(1, inner)
        def _(step):
            peer = (me + step) % inner
            in_copy(kind, peer, me).wait_send()
            out_copy(kind, peer, me).wait_send()

        @pl.loop(1, chips)
        def _(step):
            z_copy(kind, (z + step) % chips, z).wait_send()

        total_copy(kind).wait_send()
        carried_copy(kind, my_rows).wait_send()


def outputs_kernel(scale, q_ref, k_ref, v_ref, d_ref, s_ref, o_ref, gq_ref, gk_ref, gv_ref):
    rows = q_ref.shape[0]
    lower = lax.broadcasted_iota(jnp.int32, (rows, rows), 0) >= lax.broadcasted_iota(
        jnp.int32, (rows, rows), 1
    )
    for h in range(q_ref.shape[1] // HEAD):
        cols = slice(h * HEAD, (h + 1) * HEAD)
        q, k, v, d = q_ref[:, cols], k_ref[:, cols], v_ref[:, cols], d_ref[:, cols]
        s, g = s_ref[0, h], s_ref[1, h]
        a = jnp.where(lower, dot(q, k, 1, 1), 0.0).astype(jnp.bfloat16)
        b = jnp.where(lower, dot(d, v, 1, 1), 0.0).astype(jnp.bfloat16)
        o_ref[:, cols] = (scale * (dot(q, s, 1, 0) + dot(a, v, 1, 0))).astype(o_ref.dtype)
        gq_ref[:, cols] = (scale * (dot(d, s, 1, 1) + dot(b, k, 1, 0))).astype(gq_ref.dtype)
        gk_ref[:, cols] = (scale * (dot(v, g, 1, 1) + dot(b, q, 0, 0))).astype(gk_ref.dtype)
        gv_ref[:, cols] = (scale * (dot(k, g, 1, 0) + dot(a, d, 0, 0))).astype(gv_ref.dtype)


def body(queries, keys, values, cotangent):
    rows, width = queries.shape
    heads = width // HEAD
    inner, outer = lax.axis_size("inner"), lax.axis_size("outer")
    scale = float(HEAD * rows * inner * outer) ** (-0.5)
    assert inner == 2 * heads
    chips, half, quarter = outer // 2, HEAD // 2, HEAD // 4
    vmem = pl.BlockSpec(memory_space=pltpu.VMEM)
    dma = pltpu.SemaphoreType.DMA

    state = pl.pallas_call(
        functools.partial(exchange_kernel, heads, inner, outer),
        out_shape=jax.ShapeDtypeStruct((2, heads, HEAD, HEAD), jnp.bfloat16),
        in_specs=[vmem] * 4,
        out_specs=vmem,
        scratch_shapes=[
            pltpu.VMEM((2, inner, half, HEAD), jnp.bfloat16),
            pltpu.VMEM((2, inner, half, HEAD), jnp.bfloat16),
            pltpu.VMEM((2, inner, half, HEAD), jnp.float32),
            pltpu.VMEM((2, inner, half, HEAD), jnp.bfloat16),
            pltpu.VMEM((2, half, HEAD), jnp.float32),
            pltpu.VMEM((2, half, HEAD), jnp.float32),
            pltpu.VMEM((2, quarter, HEAD), jnp.bfloat16),
            pltpu.VMEM((2, chips, quarter, HEAD), jnp.bfloat16),
            pltpu.VMEM((2, half, HEAD), jnp.float32),
            dma((2, inner)), dma((2, inner)), dma((2, chips)), dma((2, chips)),
            dma((2, inner)), dma((2, inner)), dma((2, 2)), dma((2, 2)),
        ],
        compiler_params=pltpu.CompilerParams(collective_id=0, has_side_effects=True),
    )(queries, keys, values, cotangent)

    steps = 4
    tokens = pl.BlockSpec((rows, width // steps), lambda i: (0, i))
    return pl.pallas_call(
        functools.partial(outputs_kernel, scale),
        grid=(steps,),
        out_shape=(jax.ShapeDtypeStruct((rows, width), jnp.bfloat16),) * 4,
        in_specs=[tokens] * 4
        + [pl.BlockSpec((2, heads // steps, HEAD, HEAD), lambda i: (0, i, 0, 0))],
        out_specs=(tokens,) * 4,
    )(queries, keys, values, cotangent, state)


def solution(mesh):
    spec = P(("outer", "inner"), None)
    return jax.shard_map(
        body, mesh=mesh, in_specs=(spec,) * 4, out_specs=(spec,) * 4, check_vma=False
    )
```

```python
import functools

import jax
import jax.numpy as jnp
from jax import lax
from jax.experimental import pallas as pl
from jax.experimental.pallas import tpu as pltpu
from jax.sharding import PartitionSpec as P

HEAD = 128
LINE = 8
MESH = pl.DeviceIdType.MESH


def dot(a, b, over_a, over_b):
    return lax.dot_general(
        a, b, (((over_a,), (over_b,)), ((), ())), preferred_element_type=jnp.float32
    )


def roles(kind, group, y):
    w = y if kind == 0 else LINE - 1 - y
    first = (w + group) % 2 == 0
    leads = jnp.logical_or(first, w == 0)
    has_partner = jnp.logical_and(first, w < LINE - 1)
    follows = jnp.logical_and(jnp.logical_not(first), w > 0)
    return leads, has_partner, follows


def exchange_kernel(
    heads, inner, outer, q_ref, k_ref, v_ref, d_ref, state_ref,
    states, near, joined, arrived, prefix, outgoing, onward, running, total, mate, pair, pairs, carried,
    in_send, in_recv, z_send, z_recv, out_send, out_recv, core_send, core_recv,
    near_send, near_recv, on_send, on_recv,
):
    me, place = lax.axis_index("inner"), lax.axis_index("outer")
    chips, half, quarter = outer // 2, HEAD // 2, HEAD // 4
    z, core = place // 2, place % 2
    y = me % LINE
    some = heads // 2
    my_group = me % heads // some
    other = (place + 1 - 2 * core, me)
    my_rows = pl.ds(pl.multiple_of(core * quarter, quarter), quarter)
    other_rows = pl.ds(pl.multiple_of((1 - core) * quarter, quarter), quarter)

    def in_copy(kind, peer, source):
        return pltpu.make_async_remote_copy(
            joined.at[kind, peer], arrived.at[kind, source],
            in_send.at[kind, peer], in_recv.at[kind, source],
            device_id=(place, peer), device_id_type=MESH,
        )

    def z_copy(kind, peer, source):
        return pltpu.make_async_remote_copy(
            pair.at[kind], pairs.at[kind, source], z_send.at[kind, peer], z_recv.at[kind, source],
            device_id=(peer * 2 + core, me), device_id_type=MESH,
        )

    def state_at(kind, source):
        rows = pl.ds(pl.multiple_of(source // heads * half, half), half)
        return state_ref.at[kind, source % heads, rows]

    def out_copy(kind, peer, source):
        return pltpu.make_async_remote_copy(
            outgoing.at[kind, peer], state_at(kind, source),
            out_send.at[kind, peer], out_recv.at[kind, source],
            device_id=(place, peer), device_id_type=MESH,
        )

    def total_copy(kind):
        return pltpu.make_async_remote_copy(
            total.at[kind], mate.at[kind], core_send.at[0, kind], core_recv.at[0, kind],
            device_id=other, device_id_type=MESH,
        )

    def carried_copy(kind, rows):
        return pltpu.make_async_remote_copy(
            carried.at[kind, rows], carried.at[kind, rows],
            core_send.at[1, kind], core_recv.at[1, kind],
            device_id=other, device_id_type=MESH,
        )

    def make_states(kind, a_ref, b_ref):
        for h in range(heads):
            cols = slice(h * HEAD, (h + 1) * HEAD)
            both = dot(a_ref[:, cols], b_ref[:, cols], 0, 0).astype(states.dtype)
            states[kind, h] = both[:half]
            states[kind, heads + h] = both[half:]

    def near_copy(kind, group, part):
        return pltpu.make_async_remote_copy(
            states.at[kind, pl.ds(part * heads + group * some, some)], near.at[kind, part],
            near_send.at[kind, part], near_recv.at[kind, part],
            device_id=(place, (me + (inner - 1 if kind == 0 else 1)) % inner),
            device_id_type=MESH,
        )

    def on_copy(kind, group, i):
        return pltpu.make_async_remote_copy(
            onward.at[kind, i], state_ref.at[kind, group * some + i],
            on_send.at[kind, i], on_recv.at[kind, i],
            device_id=(place, (me + (1 if kind == 0 else inner - 1)) % inner),
            device_id_type=MESH,
        )

    def leads_mine(kind, source):
        return roles(kind, my_group, source % LINE)[0]

    def send_near(kind):
        for group in range(2):
            follows = roles(kind, group, y)[2]

            @pl.when(follows)
            def _():
                for part in range(2):
                    near_copy(kind, group, part).start()

    def send_joined(kind):
        for group in range(2):
            leads, has_partner, _ = roles(kind, group, y)

            @pl.when(has_partner)
            def _():
                for part in range(2):
                    near_copy(kind, group, part).wait_recv()

            @pl.when(leads)
            def _():
                @pl.loop(0, 2 * some)
                def _(step):
                    at = (me + step) % (2 * some)
                    part, i = at // some, at % some
                    peer = part * heads + group * some + i
                    mine = states[kind, peer].astype(jnp.float32)

                    @pl.when(has_partner)
                    def _():
                        both = mine + near[kind, part, i].astype(jnp.float32)
                        joined[kind, peer] = both.astype(joined.dtype)

                    @pl.when(jnp.logical_not(has_partner))
                    def _():
                        joined[kind, peer] = mine.astype(joined.dtype)

                    @pl.when(peer != me)
                    def _():
                        in_copy(kind, peer, me).start()

                    @pl.when(peer == me)
                    def _():
                        arrived[kind, me] = joined[kind, me]

    def sum_within(kind):
        total[kind] = jnp.zeros((half, HEAD), jnp.float32)

        @pl.loop(0, inner)
        def _(step):
            source = (me + inner - step) % inner

            @pl.when(leads_mine(kind, source))
            def _():
                @pl.when(source != me)
                def _():
                    in_copy(kind, source, source).wait_recv()

                total[kind] += arrived[kind, source].astype(jnp.float32)

        total_copy(kind).start()
        running[...] = jnp.zeros((half, HEAD), jnp.float32)

        @pl.loop(0, inner)
        def _(step):
            at = step if kind == 0 else inner - 1 - step

            @pl.when(leads_mine(kind, at))
            def _():
                before = running[...]
                prefix[kind, at] = before
                running[...] = before + arrived[kind, at].astype(jnp.float32)

    def send_pair(kind):
        total_copy(kind).wait_recv()
        pair[kind] = (total[kind, my_rows] + mate[kind, my_rows]).astype(pair.dtype)

        @pl.loop(1, chips)
        def _(step):
            z_copy(kind, (z + step) % chips, z).start()

    def sum_across(kind):
        def add_pair(step, acc):
            source = (z + chips - step) % chips
            z_copy(kind, source, source).wait_recv()
            reached = source < z if kind == 0 else source > z
            return acc + jnp.where(reached, pairs[kind, source].astype(jnp.float32), 0.0)

        zeros = jnp.zeros((quarter, HEAD), jnp.float32)
        carried[kind, my_rows] = lax.fori_loop(1, chips, add_pair, zeros)
        carried_copy(kind, my_rows).start()
        carried_copy(kind, other_rows).wait_recv()

    def send_sums(kind):
        offset = carried[kind] + jnp.where(core + kind == 1, mate[kind], 0.0)

        @pl.loop(0, inner)
        def _(step):
            peer = (me + step) % inner

            @pl.when(leads_mine(kind, peer))
            def _():
                whole = (prefix[kind, peer] + offset).astype(outgoing.dtype)

                @pl.when(peer != me)
                def _():
                    outgoing[kind, peer] = whole
                    out_copy(kind, peer, me).start()

                @pl.when(peer == me)
                def _():
                    state_at(kind, me)[...] = whole

    def send_onward(kind):
        for group in range(2):
            leads, has_partner, _ = roles(kind, group, y)

            @pl.when(leads)
            def _():
                @pl.loop(0, some)
                def _(i):
                    h = group * some + i
                    for part in range(2):
                        source = part * heads + h

                        @pl.when(source != me)
                        def _():
                            out_copy(kind, source, source).wait_recv()

                    @pl.when(has_partner)
                    def _():
                        for part in range(2):
                            rows = slice(part * half, (part + 1) * half)
                            onward[kind, i, rows] = (
                                state_ref[kind, h, rows].astype(jnp.float32)
                                + states[kind, part * heads + h].astype(jnp.float32)
                            ).astype(onward.dtype)
                        on_copy(kind, group, i).start()

    barrier = pltpu.get_barrier_semaphore()

    @pl.loop(1, inner)
    def _(step):
        pl.semaphore_signal(
            barrier, inc=1, device_id=(place, (me + step) % inner), device_id_type=MESH
        )

    @pl.loop(1, chips)
    def _(step):
        pl.semaphore_signal(
            barrier, inc=1, device_id=((z + step) % chips * 2 + core, me), device_id_type=MESH
        )

    pl.semaphore_signal(barrier, inc=1, device_id=other, device_id_type=MESH)
    make_states(0, k_ref, v_ref)
    pl.semaphore_wait(barrier, inner - 1 + chips - 1 + 1)
    send_near(0)
    make_states(1, q_ref, d_ref)
    send_near(1)
    for kind in range(2):
        send_joined(kind)
    for kind in range(2):
        sum_within(kind)
        send_pair(kind)
        sum_across(kind)
        send_sums(kind)
    for kind in range(2):
        send_onward(kind)
    for kind in range(2):
        for group in range(2):

            @pl.when(roles(kind, group, y)[2])
            def _():
                @pl.loop(0, some)
                def _(i):
                    on_copy(kind, group, i).wait_recv()

    for kind in range(2):
        for group in range(2):
            leads, has_partner, follows = roles(kind, group, y)

            @pl.when(follows)
            def _():
                for part in range(2):
                    near_copy(kind, group, part).wait_send()

            @pl.when(has_partner)
            def _():
                @pl.loop(0, some)
                def _(i):
                    on_copy(kind, group, i).wait_send()

            @pl.when(leads)
            def _():
                @pl.loop(0, 2 * some)
                def _(at):
                    peer = at // some * heads + group * some + at % some

                    @pl.when(peer != me)
                    def _():
                        in_copy(kind, peer, me).wait_send()

        @pl.loop(1, inner)
        def _(step):
            peer = (me + step) % inner

            @pl.when(leads_mine(kind, peer))
            def _():
                out_copy(kind, peer, me).wait_send()

        @pl.loop(1, chips)
        def _(step):
            z_copy(kind, (z + step) % chips, z).wait_send()

        total_copy(kind).wait_send()
        carried_copy(kind, my_rows).wait_send()


def outputs_kernel(scale, q_ref, k_ref, v_ref, d_ref, s_ref, o_ref, gq_ref, gk_ref, gv_ref):
    rows = q_ref.shape[0]
    lower = lax.broadcasted_iota(jnp.int32, (rows, rows), 0) >= lax.broadcasted_iota(
        jnp.int32, (rows, rows), 1
    )
    for h in range(q_ref.shape[1] // HEAD):
        cols = slice(h * HEAD, (h + 1) * HEAD)
        q, k, v, d = q_ref[:, cols], k_ref[:, cols], v_ref[:, cols], d_ref[:, cols]
        s, g = s_ref[0, h], s_ref[1, h]
        a = jnp.where(lower, dot(q, k, 1, 1), 0.0).astype(jnp.bfloat16)
        b = jnp.where(lower, dot(d, v, 1, 1), 0.0).astype(jnp.bfloat16)
        o_ref[:, cols] = (scale * (dot(q, s, 1, 0) + dot(a, v, 1, 0))).astype(o_ref.dtype)
        gq_ref[:, cols] = (scale * (dot(d, s, 1, 1) + dot(b, k, 1, 0))).astype(gq_ref.dtype)
        gk_ref[:, cols] = (scale * (dot(v, g, 1, 1) + dot(b, q, 0, 0))).astype(gk_ref.dtype)
        gv_ref[:, cols] = (scale * (dot(k, g, 1, 0) + dot(a, d, 0, 0))).astype(gv_ref.dtype)


def body(queries, keys, values, cotangent):
    rows, width = queries.shape
    heads = width // HEAD
    inner, outer = lax.axis_size("inner"), lax.axis_size("outer")
    scale = float(HEAD * rows * inner * outer) ** (-0.5)
    assert inner == 2 * heads
    chips, half, quarter, some = outer // 2, HEAD // 2, HEAD // 4, heads // 2
    vmem = pl.BlockSpec(memory_space=pltpu.VMEM)
    dma = pltpu.SemaphoreType.DMA

    state = pl.pallas_call(
        functools.partial(exchange_kernel, heads, inner, outer),
        out_shape=jax.ShapeDtypeStruct((2, heads, HEAD, HEAD), jnp.bfloat16),
        in_specs=[vmem] * 4,
        out_specs=vmem,
        scratch_shapes=[
            pltpu.VMEM((2, inner, half, HEAD), jnp.bfloat16),
            pltpu.VMEM((2, 2, some, half, HEAD), jnp.bfloat16),
            pltpu.VMEM((2, inner, half, HEAD), jnp.bfloat16),
            pltpu.VMEM((2, inner, half, HEAD), jnp.bfloat16),
            pltpu.VMEM((2, inner, half, HEAD), jnp.float32),
            pltpu.VMEM((2, inner, half, HEAD), jnp.bfloat16),
            pltpu.VMEM((2, some, HEAD, HEAD), jnp.bfloat16),
            pltpu.VMEM((half, HEAD), jnp.float32),
            pltpu.VMEM((2, half, HEAD), jnp.float32),
            pltpu.VMEM((2, half, HEAD), jnp.float32),
            pltpu.VMEM((2, quarter, HEAD), jnp.bfloat16),
            pltpu.VMEM((2, chips, quarter, HEAD), jnp.bfloat16),
            pltpu.VMEM((2, half, HEAD), jnp.float32),
            dma((2, inner)), dma((2, inner)), dma((2, chips)), dma((2, chips)),
            dma((2, inner)), dma((2, inner)), dma((2, 2)), dma((2, 2)),
            dma((2, 2)), dma((2, 2)), dma((2, some)), dma((2, some)),
        ],
        compiler_params=pltpu.CompilerParams(collective_id=0, has_side_effects=True),
    )(queries, keys, values, cotangent)

    steps = 4
    tokens = pl.BlockSpec((rows, width // steps), lambda i: (0, i))
    return pl.pallas_call(
        functools.partial(outputs_kernel, scale),
        grid=(steps,),
        out_shape=(jax.ShapeDtypeStruct((rows, width), jnp.bfloat16),) * 4,
        in_specs=[tokens] * 4
        + [pl.BlockSpec((2, heads // steps, HEAD, HEAD), lambda i: (0, i, 0, 0))],
        out_specs=(tokens,) * 4,
    )(queries, keys, values, cotangent, state)


def solution(mesh):
    spec = P(("outer", "inner"), None)
    return jax.shard_map(
        body, mesh=mesh, in_specs=(spec,) * 4, out_specs=(spec,) * 4, check_vma=False
    )
```

```python
import functools

import jax
import jax.numpy as jnp
from jax import lax
from jax.experimental import pallas as pl
from jax.experimental.pallas import tpu as pltpu
from jax.sharding import PartitionSpec as P

HEAD = 128
MESH = pl.DeviceIdType.MESH


def dot(a, b, over_a, over_b):
    return lax.dot_general(
        a, b, (((over_a,), (over_b,)), ((), ())), preferred_element_type=jnp.float32
    )


def exchange_kernel(
    heads, inner, outer, q_ref, k_ref, v_ref, d_ref, state_ref,
    states, arrived, prefix, outgoing, total, mate, pair, pairs, carried,
    in_send, in_recv, z_send, z_recv, out_send, out_recv, core_send, core_recv,
):
    me, place = lax.axis_index("inner"), lax.axis_index("outer")
    chips, half, quarter = outer // 2, HEAD // 2, HEAD // 4
    z, core = place // 2, place % 2
    other = (place + 1 - 2 * core, me)
    my_rows = pl.ds(pl.multiple_of(core * quarter, quarter), quarter)
    other_rows = pl.ds(pl.multiple_of((1 - core) * quarter, quarter), quarter)

    def in_copy(kind, peer, source):
        return pltpu.make_async_remote_copy(
            states.at[kind, peer], arrived.at[kind, source],
            in_send.at[kind], in_recv.at[kind],
            device_id=(place, peer), device_id_type=MESH,
        )

    def z_copy(kind, peer, source):
        return pltpu.make_async_remote_copy(
            pair.at[kind], pairs.at[kind, source], z_send.at[kind], z_recv.at[kind],
            device_id=(peer * 2 + core, me), device_id_type=MESH,
        )

    def state_at(kind, source):
        rows = pl.ds(pl.multiple_of(source // heads * half, half), half)
        return state_ref.at[kind, source % heads, rows]

    def out_copy(kind, peer, source):
        return pltpu.make_async_remote_copy(
            outgoing.at[kind, peer], state_at(kind, source),
            out_send.at[kind], out_recv.at[kind],
            device_id=(place, peer), device_id_type=MESH,
        )

    def all_in(kind):
        most = pl.ds(0, inner - 1)
        return pltpu.make_async_remote_copy(
            states.at[kind, most], arrived.at[kind, most], in_send.at[kind], in_recv.at[kind],
            device_id=other, device_id_type=MESH,
        )

    def all_out(kind):
        most = pl.ds(0, inner - 1)
        return pltpu.make_async_remote_copy(
            outgoing.at[kind, most], arrived.at[kind, most], out_send.at[kind], out_recv.at[kind],
            device_id=other, device_id_type=MESH,
        )

    def all_z(kind):
        most = pl.ds(0, chips - 1)
        return pltpu.make_async_remote_copy(
            pairs.at[kind, most], pairs.at[kind, most], z_send.at[kind], z_recv.at[kind],
            device_id=other, device_id_type=MESH,
        )

    def total_copy(kind):
        return pltpu.make_async_remote_copy(
            total.at[kind], mate.at[kind], core_send.at[0, kind], core_recv.at[0, kind],
            device_id=other, device_id_type=MESH,
        )

    def carried_copy(kind, rows):
        return pltpu.make_async_remote_copy(
            carried.at[kind, rows], carried.at[kind, rows],
            core_send.at[1, kind], core_recv.at[1, kind],
            device_id=other, device_id_type=MESH,
        )

    def make_states(kind, a_ref, b_ref):
        for h in range(heads):
            cols = slice(h * HEAD, (h + 1) * HEAD)
            both = dot(a_ref[:, cols], b_ref[:, cols], 0, 0).astype(states.dtype)
            states[kind, h] = both[:half]
            states[kind, heads + h] = both[half:]

    def send_states(kind):
        for step in range(1, inner):
            in_copy(kind, lax.rem(me + step, inner), me).start()

        arrived[kind, me] = states[kind, me]

    def sum_within(kind):
        all_in(kind).wait_recv()
        acc = jnp.zeros((half, HEAD), jnp.float32)
        for step in range(inner):
            at = step if kind == 0 else inner - 1 - step
            prefix[kind, at] = acc
            acc = acc + arrived[kind, at].astype(jnp.float32)
        total[kind] = acc
        total_copy(kind).start()

    def send_pair(kind):
        total_copy(kind).wait_recv()
        pair[kind] = (total[kind, my_rows] + mate[kind, my_rows]).astype(pair.dtype)

        for step in range(1, chips):
            z_copy(kind, lax.rem(z + step, chips), z).start()

    def sum_across(kind):
        all_z(kind).wait_recv()
        acc = jnp.zeros((quarter, HEAD), jnp.float32)
        for source in range(chips):
            reached = source < z if kind == 0 else source > z
            acc = acc + jnp.where(reached, pairs[kind, source].astype(jnp.float32), 0.0)
        carried[kind, my_rows] = acc
        carried_copy(kind, my_rows).start()
        carried_copy(kind, other_rows).wait_recv()

    def send_sums(kind):
        offset = carried[kind] + jnp.where(core + kind == 1, mate[kind], 0.0)

        for peer in range(inner):
            outgoing[kind, peer] = (prefix[kind, peer] + offset).astype(outgoing.dtype)

        for step in range(1, inner):
            out_copy(kind, lax.rem(me + step, inner), me).start()

        state_at(kind, me)[...] = (prefix[kind, me] + offset).astype(outgoing.dtype)

    barrier = pltpu.get_barrier_semaphore()

    for step in range(1, inner):
        peer = (place, lax.rem(me + step, inner))
        pl.semaphore_signal(barrier, inc=1, device_id=peer, device_id_type=MESH)

    for step in range(1, chips):
        peer = (lax.rem(z + step, chips) * 2 + core, me)
        pl.semaphore_signal(barrier, inc=1, device_id=peer, device_id_type=MESH)

    pl.semaphore_signal(barrier, inc=1, device_id=other, device_id_type=MESH)
    make_states(0, k_ref, v_ref)
    pl.semaphore_wait(barrier, inner - 1 + chips - 1 + 1)
    send_states(0)
    make_states(1, q_ref, d_ref)
    send_states(1)
    for kind in range(2):
        sum_within(kind)
        send_pair(kind)
        sum_across(kind)
        send_sums(kind)

    for kind in range(2):
        all_in(kind).wait_send()
        all_z(kind).wait_send()
        total_copy(kind).wait_send()
        carried_copy(kind, my_rows).wait_send()

    for kind in range(2):
        all_out(kind).wait_send()
        all_out(kind).wait_recv()


def outputs_kernel(scale, q_ref, k_ref, v_ref, d_ref, s_ref, o_ref, gq_ref, gk_ref, gv_ref):
    rows = q_ref.shape[0]
    lower = lax.broadcasted_iota(jnp.int32, (rows, rows), 0) >= lax.broadcasted_iota(
        jnp.int32, (rows, rows), 1
    )
    for h in range(q_ref.shape[1] // HEAD):
        cols = slice(h * HEAD, (h + 1) * HEAD)
        q, k, v, d = q_ref[:, cols], k_ref[:, cols], v_ref[:, cols], d_ref[:, cols]
        s, g = s_ref[0, h], s_ref[1, h]
        a = jnp.where(lower, dot(q, k, 1, 1), 0.0).astype(jnp.bfloat16)
        b = jnp.where(lower, dot(d, v, 1, 1), 0.0).astype(jnp.bfloat16)
        o_ref[:, cols] = (scale * (dot(q, s, 1, 0) + dot(a, v, 1, 0))).astype(o_ref.dtype)
        gq_ref[:, cols] = (scale * (dot(d, s, 1, 1) + dot(b, k, 1, 0))).astype(gq_ref.dtype)
        gk_ref[:, cols] = (scale * (dot(v, g, 1, 1) + dot(b, q, 0, 0))).astype(gk_ref.dtype)
        gv_ref[:, cols] = (scale * (dot(k, g, 1, 0) + dot(a, d, 0, 0))).astype(gv_ref.dtype)


def body(queries, keys, values, cotangent):
    rows, width = queries.shape
    heads = width // HEAD
    inner, outer = lax.axis_size("inner"), lax.axis_size("outer")
    scale = float(HEAD * rows * inner * outer) ** (-0.5)
    assert inner == 2 * heads
    chips, half, quarter = outer // 2, HEAD // 2, HEAD // 4
    vmem = pl.BlockSpec(memory_space=pltpu.VMEM)
    dma = pltpu.SemaphoreType.DMA

    state = pl.pallas_call(
        functools.partial(exchange_kernel, heads, inner, outer),
        out_shape=jax.ShapeDtypeStruct((2, heads, HEAD, HEAD), jnp.bfloat16),
        in_specs=[vmem] * 4,
        out_specs=vmem,
        scratch_shapes=[
            pltpu.VMEM((2, inner, half, HEAD), jnp.bfloat16),
            pltpu.VMEM((2, inner, half, HEAD), jnp.bfloat16),
            pltpu.VMEM((2, inner, half, HEAD), jnp.float32),
            pltpu.VMEM((2, inner, half, HEAD), jnp.bfloat16),
            pltpu.VMEM((2, half, HEAD), jnp.float32),
            pltpu.VMEM((2, half, HEAD), jnp.float32),
            pltpu.VMEM((2, quarter, HEAD), jnp.bfloat16),
            pltpu.VMEM((2, chips, quarter, HEAD), jnp.bfloat16),
            pltpu.VMEM((2, half, HEAD), jnp.float32),
            dma((2,)), dma((2,)), dma((2,)), dma((2,)),
            dma((2,)), dma((2,)), dma((2, 2)), dma((2, 2)),
        ],
        compiler_params=pltpu.CompilerParams(collective_id=0, has_side_effects=True),
    )(queries, keys, values, cotangent)

    steps = 4
    tokens = pl.BlockSpec((rows, width // steps), lambda i: (0, i))
    return pl.pallas_call(
        functools.partial(outputs_kernel, scale),
        grid=(steps,),
        out_shape=(jax.ShapeDtypeStruct((rows, width), jnp.bfloat16),) * 4,
        in_specs=[tokens] * 4
        + [pl.BlockSpec((2, heads // steps, HEAD, HEAD), lambda i: (0, i, 0, 0))],
        out_specs=(tokens,) * 4,
    )(queries, keys, values, cotangent, state)


def solution(mesh):
    spec = P(("outer", "inner"), None)
    return jax.shard_map(
        body, mesh=mesh, in_specs=(spec,) * 4, out_specs=(spec,) * 4, check_vma=False
    )
```

```python
import functools

import jax
import jax.numpy as jnp
from jax import lax
from jax.experimental import pallas as pl
from jax.experimental.pallas import tpu as pltpu
from jax.sharding import PartitionSpec as P

HEAD = 128
MESH = pl.DeviceIdType.MESH


def dot(a, b, over_a, over_b):
    return lax.dot_general(
        a, b, (((over_a,), (over_b,)), ((), ())), preferred_element_type=jnp.float32
    )


def exchange_kernel(
    heads, inner, outer, scale, q_ref, k_ref, v_ref, d_ref,
    o_out, gq_out, part_k_out, part_v_out, g_ref,
    s_ref, o_ref, gq_ref, part_k_ref, part_v_ref, put, states, arrived, prefix, outgoing, total, mate, pair, pairs, carried,
    in_send, in_recv, z_send, z_recv, out_send, out_recv, core_send, core_recv,
):
    me, place = lax.axis_index("inner"), lax.axis_index("outer")
    chips, half, quarter = outer // 2, HEAD // 2, HEAD // 4
    z, core = place // 2, place % 2
    other = (place + 1 - 2 * core, me)
    my_rows = pl.ds(pl.multiple_of(core * quarter, quarter), quarter)
    other_rows = pl.ds(pl.multiple_of((1 - core) * quarter, quarter), quarter)

    def in_copy(kind, peer, source):
        return pltpu.make_async_remote_copy(
            states.at[kind, peer], arrived.at[kind, source],
            in_send.at[kind], in_recv.at[kind],
            device_id=(place, peer), device_id_type=MESH,
        )

    def z_copy(kind, peer, source):
        return pltpu.make_async_remote_copy(
            pair.at[kind], pairs.at[kind, source], z_send.at[kind], z_recv.at[kind],
            device_id=(peer * 2 + core, me), device_id_type=MESH,
        )

    def state_at(kind, source):
        rows = pl.ds(pl.multiple_of(source // heads * half, half), half)
        return (s_ref, g_ref)[kind].at[source % heads, rows]

    def out_copy(kind, peer, source):
        return pltpu.make_async_remote_copy(
            outgoing.at[kind, peer], state_at(kind, source),
            out_send.at[kind], out_recv.at[kind],
            device_id=(place, peer), device_id_type=MESH,
        )

    def all_in(kind):
        most = pl.ds(0, inner - 1)
        return pltpu.make_async_remote_copy(
            states.at[kind, most], arrived.at[kind, most], in_send.at[kind], in_recv.at[kind],
            device_id=other, device_id_type=MESH,
        )

    def all_out(kind):
        most = pl.ds(0, inner - 1)
        return pltpu.make_async_remote_copy(
            outgoing.at[kind, most], arrived.at[kind, most], out_send.at[kind], out_recv.at[kind],
            device_id=other, device_id_type=MESH,
        )

    def all_z(kind):
        most = pl.ds(0, chips - 1)
        return pltpu.make_async_remote_copy(
            pairs.at[kind, most], pairs.at[kind, most], z_send.at[kind], z_recv.at[kind],
            device_id=other, device_id_type=MESH,
        )

    def total_copy(kind):
        return pltpu.make_async_remote_copy(
            total.at[kind], mate.at[kind], core_send.at[0, kind], core_recv.at[0, kind],
            device_id=other, device_id_type=MESH,
        )

    def carried_copy(kind, rows):
        return pltpu.make_async_remote_copy(
            carried.at[kind, rows], carried.at[kind, rows],
            core_send.at[1, kind], core_recv.at[1, kind],
            device_id=other, device_id_type=MESH,
        )

    def make_states(kind, a_ref, b_ref):
        for h in range(heads):
            cols = slice(h * HEAD, (h + 1) * HEAD)
            both = dot(a_ref[:, cols], b_ref[:, cols], 0, 0).astype(states.dtype)
            states[kind, h] = both[:half]
            states[kind, heads + h] = both[half:]

    def send_states(kind):
        for step in range(1, inner):
            in_copy(kind, lax.rem(me + step, inner), me).start()

        arrived[kind, me] = states[kind, me]

    def sum_within(kind):
        all_in(kind).wait_recv()
        acc = jnp.zeros((half, HEAD), jnp.float32)
        for step in range(inner):
            at = step if kind == 0 else inner - 1 - step
            prefix[kind, at] = acc
            acc = acc + arrived[kind, at].astype(jnp.float32)
        total[kind] = acc
        total_copy(kind).start()

    def send_pair(kind):
        total_copy(kind).wait_recv()
        pair[kind] = (total[kind, my_rows] + mate[kind, my_rows]).astype(pair.dtype)

        for step in range(1, chips):
            z_copy(kind, lax.rem(z + step, chips), z).start()

    def sum_across(kind):
        all_z(kind).wait_recv()
        acc = jnp.zeros((quarter, HEAD), jnp.float32)
        for source in range(chips):
            reached = source < z if kind == 0 else source > z
            acc = acc + jnp.where(reached, pairs[kind, source].astype(jnp.float32), 0.0)
        carried[kind, my_rows] = acc
        carried_copy(kind, my_rows).start()
        carried_copy(kind, other_rows).wait_recv()

    def send_sums(kind):
        offset = carried[kind] + jnp.where(core + kind == 1, mate[kind], 0.0)

        for peer in range(inner):
            outgoing[kind, peer] = (prefix[kind, peer] + offset).astype(outgoing.dtype)

        for step in range(1, inner):
            out_copy(kind, lax.rem(me + step, inner), me).start()

        state_at(kind, me)[...] = (prefix[kind, me] + offset).astype(outgoing.dtype)

    def use_sums_before():
        rows = q_ref.shape[0]
        lower = lax.broadcasted_iota(jnp.int32, (rows, rows), 0) >= lax.broadcasted_iota(
            jnp.int32, (rows, rows), 1
        )
        for h in range(heads):
            cols = slice(h * HEAD, (h + 1) * HEAD)
            q, k, v, d = q_ref[:, cols], k_ref[:, cols], v_ref[:, cols], d_ref[:, cols]
            s = s_ref[h]
            a = jnp.where(lower, dot(q, k, 1, 1), 0.0).astype(jnp.bfloat16)
            b = jnp.where(lower, dot(d, v, 1, 1), 0.0).astype(jnp.bfloat16)
            o_ref[:, cols] = (scale * (dot(q, s, 1, 0) + dot(a, v, 1, 0))).astype(o_ref.dtype)
            gq_ref[:, cols] = (scale * (dot(d, s, 1, 1) + dot(b, k, 1, 0))).astype(gq_ref.dtype)
            part_k_ref[:, cols] = dot(b, q, 0, 0)
            part_v_ref[:, cols] = dot(a, d, 0, 0)

    puts = [
        pltpu.make_async_copy(here, there, put.at[i])
        for i, (here, there) in enumerate(
            ((o_ref, o_out), (gq_ref, gq_out), (part_k_ref, part_k_out), (part_v_ref, part_v_out))
        )
    ]

    barrier = pltpu.get_barrier_semaphore()

    for step in range(1, inner):
        peer = (place, lax.rem(me + step, inner))
        pl.semaphore_signal(barrier, inc=1, device_id=peer, device_id_type=MESH)

    for step in range(1, chips):
        peer = (lax.rem(z + step, chips) * 2 + core, me)
        pl.semaphore_signal(barrier, inc=1, device_id=peer, device_id_type=MESH)

    pl.semaphore_signal(barrier, inc=1, device_id=other, device_id_type=MESH)
    make_states(0, k_ref, v_ref)
    pl.semaphore_wait(barrier, inner - 1 + chips - 1 + 1)
    send_states(0)
    make_states(1, q_ref, d_ref)
    send_states(1)
    for kind in range(2):
        sum_within(kind)
        send_pair(kind)
        sum_across(kind)
        send_sums(kind)

    for kind in range(2):
        all_in(kind).wait_send()
        all_z(kind).wait_send()
        total_copy(kind).wait_send()
        carried_copy(kind, my_rows).wait_send()

    all_out(0).wait_send()
    all_out(0).wait_recv()
    use_sums_before()
    for copy in puts:
        copy.start()
    all_out(1).wait_send()
    for copy in puts:
        copy.wait()
    all_out(1).wait_recv()


def outputs_kernel(
    scale, k_ref, v_ref, o_in, gq_in, part_k_ref, part_v_ref, g_ref, o_ref, gq_ref, gk_ref, gv_ref
):
    o_ref[...] = o_in[...]
    gq_ref[...] = gq_in[...]
    for h in range(k_ref.shape[1] // HEAD):
        cols = slice(h * HEAD, (h + 1) * HEAD)
        k, v, g = k_ref[:, cols], v_ref[:, cols], g_ref[h]
        gk_ref[:, cols] = (scale * (dot(v, g, 1, 1) + part_k_ref[:, cols])).astype(gk_ref.dtype)
        gv_ref[:, cols] = (scale * (dot(k, g, 1, 0) + part_v_ref[:, cols])).astype(gv_ref.dtype)


def body(queries, keys, values, cotangent):
    rows, width = queries.shape
    heads = width // HEAD
    inner, outer = lax.axis_size("inner"), lax.axis_size("outer")
    scale = float(HEAD * rows * inner * outer) ** (-0.5)
    assert inner == 2 * heads
    chips, half, quarter = outer // 2, HEAD // 2, HEAD // 4
    vmem = pl.BlockSpec(memory_space=pltpu.VMEM)
    dma = pltpu.SemaphoreType.DMA

    narrow = jax.ShapeDtypeStruct((rows, width), jnp.bfloat16)
    wide = jax.ShapeDtypeStruct((rows, width), jnp.float32)
    anywhere = pl.BlockSpec(memory_space=pl.ANY)
    attended, grad_q, part_k, part_v, later = pl.pallas_call(
        functools.partial(exchange_kernel, heads, inner, outer, scale),
        out_shape=(
            narrow, narrow, wide, wide, jax.ShapeDtypeStruct((heads, HEAD, HEAD), jnp.bfloat16)
        ),
        in_specs=[vmem] * 4,
        out_specs=(anywhere,) * 4 + (vmem,),
        scratch_shapes=[
            pltpu.VMEM((heads, HEAD, HEAD), jnp.bfloat16),
            pltpu.VMEM((rows, width), jnp.bfloat16),
            pltpu.VMEM((rows, width), jnp.bfloat16),
            pltpu.VMEM((rows, width), jnp.float32),
            pltpu.VMEM((rows, width), jnp.float32),
            dma((4,)),
            pltpu.VMEM((2, inner, half, HEAD), jnp.bfloat16),
            pltpu.VMEM((2, inner, half, HEAD), jnp.bfloat16),
            pltpu.VMEM((2, inner, half, HEAD), jnp.float32),
            pltpu.VMEM((2, inner, half, HEAD), jnp.bfloat16),
            pltpu.VMEM((2, half, HEAD), jnp.float32),
            pltpu.VMEM((2, half, HEAD), jnp.float32),
            pltpu.VMEM((2, quarter, HEAD), jnp.bfloat16),
            pltpu.VMEM((2, chips, quarter, HEAD), jnp.bfloat16),
            pltpu.VMEM((2, half, HEAD), jnp.float32),
            dma((2,)), dma((2,)), dma((2,)), dma((2,)),
            dma((2,)), dma((2,)), dma((2, 2)), dma((2, 2)),
        ],
        compiler_params=pltpu.CompilerParams(collective_id=0, has_side_effects=True),
    )(queries, keys, values, cotangent)

    steps = 4
    tokens = pl.BlockSpec((rows, width // steps), lambda i: (0, i))
    return pl.pallas_call(
        functools.partial(outputs_kernel, scale),
        grid=(steps,),
        out_shape=(narrow,) * 4,
        in_specs=[tokens] * 6 + [pl.BlockSpec((heads // steps, HEAD, HEAD), lambda i: (i, 0, 0))],
        out_specs=(tokens,) * 4,
    )(keys, values, attended, grad_q, part_k, part_v, later)


def solution(mesh):
    spec = P(("outer", "inner"), None)
    return jax.shard_map(
        body, mesh=mesh, in_specs=(spec,) * 4, out_specs=(spec,) * 4, check_vma=False
    )
```

```python
import functools

import jax
import jax.numpy as jnp
from jax import lax
from jax.experimental import pallas as pl
from jax.experimental.pallas import tpu as pltpu
from jax.sharding import PartitionSpec as P

HEAD = 128
MESH = pl.DeviceIdType.MESH


def dot(a, b, over_a, over_b):
    return lax.dot_general(
        a, b, (((over_a,), (over_b,)), ((), ())), preferred_element_type=jnp.float32
    )


def exchange_kernel(
    heads, inner, outer, scale, q_in, k_in, v_in, d_in,
    o_out, gq_out, part_k_out, part_v_out, g_ref,
    q_ref, k_ref, v_ref, d_ref, get,
    s_ref, o_ref, gq_ref, part_k_ref, part_v_ref, put, states, arrived, prefix, outgoing, total, mate, pair, pairs, carried,
    in_send, in_recv, z_send, z_recv, out_send, out_recv, core_send, core_recv,
):
    me, place = lax.axis_index("inner"), lax.axis_index("outer")
    chips, half, quarter = outer // 2, HEAD // 2, HEAD // 4
    z, core = place // 2, place % 2
    other = (place + 1 - 2 * core, me)
    my_rows = pl.ds(pl.multiple_of(core * quarter, quarter), quarter)
    other_rows = pl.ds(pl.multiple_of((1 - core) * quarter, quarter), quarter)

    def in_copy(kind, peer, source):
        return pltpu.make_async_remote_copy(
            states.at[kind, peer], arrived.at[kind, source],
            in_send.at[kind], in_recv.at[kind],
            device_id=(place, peer), device_id_type=MESH,
        )

    def z_copy(kind, peer, source):
        return pltpu.make_async_remote_copy(
            pair.at[kind], pairs.at[kind, source], z_send.at[kind], z_recv.at[kind],
            device_id=(peer * 2 + core, me), device_id_type=MESH,
        )

    def state_at(kind, source):
        rows = pl.ds(pl.multiple_of(source // heads * half, half), half)
        return (s_ref, g_ref)[kind].at[source % heads, rows]

    def out_copy(kind, peer, source):
        return pltpu.make_async_remote_copy(
            outgoing.at[kind, peer], state_at(kind, source),
            out_send.at[kind], out_recv.at[kind],
            device_id=(place, peer), device_id_type=MESH,
        )

    def all_in(kind):
        most = pl.ds(0, inner - 1)
        return pltpu.make_async_remote_copy(
            states.at[kind, most], arrived.at[kind, most], in_send.at[kind], in_recv.at[kind],
            device_id=other, device_id_type=MESH,
        )

    def all_out(kind):
        most = pl.ds(0, inner - 1)
        return pltpu.make_async_remote_copy(
            outgoing.at[kind, most], arrived.at[kind, most], out_send.at[kind], out_recv.at[kind],
            device_id=other, device_id_type=MESH,
        )

    def all_z(kind):
        most = pl.ds(0, chips - 1)
        return pltpu.make_async_remote_copy(
            pairs.at[kind, most], pairs.at[kind, most], z_send.at[kind], z_recv.at[kind],
            device_id=other, device_id_type=MESH,
        )

    def total_copy(kind):
        return pltpu.make_async_remote_copy(
            total.at[kind], mate.at[kind], core_send.at[0, kind], core_recv.at[0, kind],
            device_id=other, device_id_type=MESH,
        )

    def carried_copy(kind, rows):
        return pltpu.make_async_remote_copy(
            carried.at[kind, rows], carried.at[kind, rows],
            core_send.at[1, kind], core_recv.at[1, kind],
            device_id=other, device_id_type=MESH,
        )

    def make_states(kind, a_ref, b_ref):
        for h in range(heads):
            cols = slice(h * HEAD, (h + 1) * HEAD)
            both = dot(a_ref[:, cols], b_ref[:, cols], 0, 0).astype(states.dtype)
            states[kind, h] = both[:half]
            states[kind, heads + h] = both[half:]

    def send_states(kind):
        for step in range(1, inner):
            in_copy(kind, lax.rem(me + step, inner), me).start()

        arrived[kind, me] = states[kind, me]

    def sum_within(kind):
        all_in(kind).wait_recv()
        acc = jnp.zeros((half, HEAD), jnp.float32)
        for step in range(inner):
            at = step if kind == 0 else inner - 1 - step
            prefix[kind, at] = acc
            acc = acc + arrived[kind, at].astype(jnp.float32)
        total[kind] = acc
        total_copy(kind).start()

    def send_pair(kind):
        total_copy(kind).wait_recv()
        pair[kind] = (total[kind, my_rows] + mate[kind, my_rows]).astype(pair.dtype)

        for step in range(1, chips):
            z_copy(kind, lax.rem(z + step, chips), z).start()

    def sum_across(kind):
        all_z(kind).wait_recv()
        acc = jnp.zeros((quarter, HEAD), jnp.float32)
        for source in range(chips):
            reached = source < z if kind == 0 else source > z
            acc = acc + jnp.where(reached, pairs[kind, source].astype(jnp.float32), 0.0)
        carried[kind, my_rows] = acc
        carried_copy(kind, my_rows).start()
        carried_copy(kind, other_rows).wait_recv()

    def send_sums(kind):
        offset = carried[kind] + jnp.where(core + kind == 1, mate[kind], 0.0)

        for peer in range(inner):
            outgoing[kind, peer] = (prefix[kind, peer] + offset).astype(outgoing.dtype)

        for step in range(1, inner):
            out_copy(kind, lax.rem(me + step, inner), me).start()

        state_at(kind, me)[...] = (prefix[kind, me] + offset).astype(outgoing.dtype)

    def use_sums_before():
        rows = q_ref.shape[0]
        lower = lax.broadcasted_iota(jnp.int32, (rows, rows), 0) >= lax.broadcasted_iota(
            jnp.int32, (rows, rows), 1
        )
        for h in range(heads):
            cols = slice(h * HEAD, (h + 1) * HEAD)
            q, k, v, d = q_ref[:, cols], k_ref[:, cols], v_ref[:, cols], d_ref[:, cols]
            s = s_ref[h]
            a = jnp.where(lower, dot(q, k, 1, 1), 0.0).astype(jnp.bfloat16)
            b = jnp.where(lower, dot(d, v, 1, 1), 0.0).astype(jnp.bfloat16)
            o_ref[:, cols] = (scale * (dot(q, s, 1, 0) + dot(a, v, 1, 0))).astype(o_ref.dtype)
            gq_ref[:, cols] = (scale * (dot(d, s, 1, 1) + dot(b, k, 1, 0))).astype(gq_ref.dtype)
            part_k_ref[:, cols] = dot(b, q, 0, 0)
            part_v_ref[:, cols] = dot(a, d, 0, 0)

    puts = [
        pltpu.make_async_copy(here, there, put.at[i])
        for i, (here, there) in enumerate(
            ((o_ref, o_out), (gq_ref, gq_out), (part_k_ref, part_k_out), (part_v_ref, part_v_out))
        )
    ]

    gets = [
        pltpu.make_async_copy(there, here, get.at[i])
        for i, (there, here) in enumerate(
            ((k_in, k_ref), (v_in, v_ref), (q_in, q_ref), (d_in, d_ref))
        )
    ]
    for copy in gets:
        copy.start()

    barrier = pltpu.get_barrier_semaphore()

    for step in range(1, inner):
        peer = (place, lax.rem(me + step, inner))
        pl.semaphore_signal(barrier, inc=1, device_id=peer, device_id_type=MESH)

    for step in range(1, chips):
        peer = (lax.rem(z + step, chips) * 2 + core, me)
        pl.semaphore_signal(barrier, inc=1, device_id=peer, device_id_type=MESH)

    pl.semaphore_signal(barrier, inc=1, device_id=other, device_id_type=MESH)
    for copy in gets[:2]:
        copy.wait()
    make_states(0, k_ref, v_ref)
    pl.semaphore_wait(barrier, inner - 1 + chips - 1 + 1)
    send_states(0)
    for copy in gets[2:]:
        copy.wait()
    make_states(1, q_ref, d_ref)
    send_states(1)
    for kind in range(2):
        sum_within(kind)
        send_pair(kind)
        sum_across(kind)
        send_sums(kind)

    for kind in range(2):
        all_in(kind).wait_send()
        all_z(kind).wait_send()
        total_copy(kind).wait_send()
        carried_copy(kind, my_rows).wait_send()

    all_out(0).wait_send()
    all_out(0).wait_recv()
    use_sums_before()
    for copy in puts:
        copy.start()
    all_out(1).wait_send()
    for copy in puts:
        copy.wait()
    all_out(1).wait_recv()


def outputs_kernel(
    scale, k_ref, v_ref, o_in, gq_in, part_k_ref, part_v_ref, g_ref, o_ref, gq_ref, gk_ref, gv_ref
):
    o_ref[...] = o_in[...]
    gq_ref[...] = gq_in[...]
    for h in range(k_ref.shape[1] // HEAD):
        cols = slice(h * HEAD, (h + 1) * HEAD)
        k, v, g = k_ref[:, cols], v_ref[:, cols], g_ref[h]
        gk_ref[:, cols] = (scale * (dot(v, g, 1, 1) + part_k_ref[:, cols])).astype(gk_ref.dtype)
        gv_ref[:, cols] = (scale * (dot(k, g, 1, 0) + part_v_ref[:, cols])).astype(gv_ref.dtype)


def body(queries, keys, values, cotangent):
    rows, width = queries.shape
    heads = width // HEAD
    inner, outer = lax.axis_size("inner"), lax.axis_size("outer")
    scale = float(HEAD * rows * inner * outer) ** (-0.5)
    assert inner == 2 * heads
    chips, half, quarter = outer // 2, HEAD // 2, HEAD // 4
    vmem = pl.BlockSpec(memory_space=pltpu.VMEM)
    dma = pltpu.SemaphoreType.DMA

    narrow = jax.ShapeDtypeStruct((rows, width), jnp.bfloat16)
    wide = jax.ShapeDtypeStruct((rows, width), jnp.float32)
    anywhere = pl.BlockSpec(memory_space=pl.ANY)
    attended, grad_q, part_k, part_v, later = pl.pallas_call(
        functools.partial(exchange_kernel, heads, inner, outer, scale),
        out_shape=(
            narrow, narrow, wide, wide, jax.ShapeDtypeStruct((heads, HEAD, HEAD), jnp.bfloat16)
        ),
        in_specs=[anywhere] * 4,
        out_specs=(anywhere,) * 4 + (vmem,),
        scratch_shapes=[pltpu.VMEM((rows, width), jnp.bfloat16)] * 4
        + [
            dma((4,)),
            pltpu.VMEM((heads, HEAD, HEAD), jnp.bfloat16),
            pltpu.VMEM((rows, width), jnp.bfloat16),
            pltpu.VMEM((rows, width), jnp.bfloat16),
            pltpu.VMEM((rows, width), jnp.float32),
            pltpu.VMEM((rows, width), jnp.float32),
            dma((4,)),
            pltpu.VMEM((2, inner, half, HEAD), jnp.bfloat16),
            pltpu.VMEM((2, inner, half, HEAD), jnp.bfloat16),
            pltpu.VMEM((2, inner, half, HEAD), jnp.float32),
            pltpu.VMEM((2, inner, half, HEAD), jnp.bfloat16),
            pltpu.VMEM((2, half, HEAD), jnp.float32),
            pltpu.VMEM((2, half, HEAD), jnp.float32),
            pltpu.VMEM((2, quarter, HEAD), jnp.bfloat16),
            pltpu.VMEM((2, chips, quarter, HEAD), jnp.bfloat16),
            pltpu.VMEM((2, half, HEAD), jnp.float32),
            dma((2,)), dma((2,)), dma((2,)), dma((2,)),
            dma((2,)), dma((2,)), dma((2, 2)), dma((2, 2)),
        ],
        compiler_params=pltpu.CompilerParams(collective_id=0, has_side_effects=True),
    )(queries, keys, values, cotangent)

    steps = 4
    tokens = pl.BlockSpec((rows, width // steps), lambda i: (0, i))
    return pl.pallas_call(
        functools.partial(outputs_kernel, scale),
        grid=(steps,),
        out_shape=(narrow,) * 4,
        in_specs=[tokens] * 6 + [pl.BlockSpec((heads // steps, HEAD, HEAD), lambda i: (i, 0, 0))],
        out_specs=(tokens,) * 4,
    )(keys, values, attended, grad_q, part_k, part_v, later)


def solution(mesh):
    spec = P(("outer", "inner"), None)
    return jax.shard_map(
        body, mesh=mesh, in_specs=(spec,) * 4, out_specs=(spec,) * 4, check_vma=False
    )
```
